128 devices in a mesh: dp: 2 (over y_hi), blk: 8 (over z, core), uly: 8 (over y_lo, x).
Axes of the slice: x: 4, y: 4 (y_hi: 2, y_lo: 2; y = y_hi * 2 + y_lo), z: 4, core: 2. Of those that a mesh axis runs over, the one named last changes fastest.
Arguments:
- hidden_states: bfloat16 [2, 16384, 4096], P('dp', ('blk', 'uly')), may hold values from -96 to 96
- block_table: int32 [2, 32, 32], P('dp'), may hold values from 0 to 1, as said below
- w_query: bfloat16 [4096, 2048], P(('dp', 'blk'), 'uly'), may hold values from -0.09375 to 0.09375
- w_key: bfloat16 [4096, 512], P(('dp', 'blk'), 'uly'), may hold values from -0.09375 to 0.09375
- w_value: bfloat16 [4096, 512], P(('dp', 'blk'), 'uly'), may hold values from -0.09375 to 0.09375
Outputs:
- attended: bfloat16 [2, 16384, 2048], P('dp', ('blk', 'uly'))
The draws below stay inside these ranges and needn't reach their ends.
Inputs may be any that keep to these rules, and one draw needn't show every extreme that they name: block_table[s, i, j] is 1 where query block i of sequence s may read key block j, else 0; it is 1 on the diagonal and 0 above it; below the diagonal a block is allowed when it lies within a window of 1 to 4 blocks ending at i, or is one of the sequence's global key blocks; the global key blocks are block 0 and exactly 8 others.
All inputs are finite; a program needn't handle non-finite values.
Results may differ from the reference program's by a relative error of at most 0.024.
The reference program's roundings to bfloat16 on the way count: a program that leaves them out, or rounds other values in their place, can miss the bound.
Values may be sent and summed in bfloat16 or wider, within the bound.
No kernel may reach another device: no remote copies, remote signals or barrier semaphores. Data moves between devices by JAX's collectives and lax.ppermute only.
A program may use at most 128 MiB of HBM per device.

```python
import jax
import jax.numpy as jnp
from jax import lax

D = 4096
H = 16
KV = 4
HD = 128
MBLK = 512
WIN = 4
SEQ = 16384
BATCH = 2
NBM = 32


def draw_hidden_states(key, part):
    base_key = jax.random.fold_in(jax.random.fold_in(key, 11), 0)
    values = jax.random.normal(base_key, (BATCH, SEQ, D), jnp.float32)
    return jnp.clip(values, -96.0, 96.0).astype(jnp.bfloat16)


def draw_block_table(key, part):
    global_key, window_key = jax.random.split(jax.random.fold_in(key, 23))
    block_count = NBM
    glob_count = min(8, block_count // 4)
    seq_keys = jax.random.split(global_key, BATCH)
    perms = jax.vmap(lambda one_key: jax.random.permutation(one_key, block_count - 1))(seq_keys) + 1
    chosen = perms[:, :glob_count]
    col_ids = jnp.arange(block_count)
    global_cols = jnp.any(col_ids[None, None, :] == chosen[:, :, None], axis=1) | (col_ids == 0)[None, :]
    global_cols = global_cols[:, None, :]
    window = jax.random.randint(window_key, (BATCH, block_count, 1), 1, WIN + 1)
    row_ids = jnp.arange(block_count)[:, None]
    col_grid = col_ids[None, :]
    allowed = (col_grid <= row_ids)[None] & (((row_ids - col_grid)[None] < window) | global_cols)
    return allowed.astype(jnp.int32)


def block_levels(rng, dims, cuts, smallest, largest):
    def one(axis_at, blocks):
        heights = jax.random.uniform(jax.random.fold_in(jax.random.fold_in(rng, 6), axis_at), (blocks,), jnp.float32, smallest / len(cuts), largest / len(cuts))
        return jnp.repeat(jnp.exp(heights), dims[axis_at] // blocks).reshape((-1,) + (1,) * (len(dims) - axis_at - 1))

    gain = one(*cuts[0])
    for cut in cuts[1:]:
        gain = gain * one(*cut)
    return gain


def centred(rng, extent, spread, bound, cuts=(), kind=jnp.bfloat16):
    drawn = jax.random.normal(rng, extent, jnp.float32) * spread
    if len(cuts) > 0:
        drawn = block_levels(rng, extent, cuts, -0.22, 0.18) * drawn
    return jnp.clip(drawn, min=-bound, max=bound).astype(kind)


def setup_inputs(seed: int = 0) -> dict:
    key_of = jax.random.split(jax.random.key(seed), 6)
    hidden_states = draw_hidden_states(jax.random.fold_in(key_of[5], 71), 0)
    block_table = draw_block_table(jax.random.fold_in(key_of[5], 71), 0)
    w_query = centred(key_of[2], (D, H * HD), D ** -0.5, 0.09375, ((0, 16), (1, 8)))
    w_key = centred(key_of[3], (D, KV * HD), D ** -0.5, 0.09375, ((0, 16), (1, 8)))
    w_value = centred(key_of[4], (D, KV * HD), D ** -0.5, 0.09375, ((0, 16), (1, 8)))
    return {"hidden_states": hidden_states, "block_table": block_table, "w_query": w_query, "w_key": w_key, "w_value": w_value}


THETA_BASE = 500000.0


def rotate(values, positions):
    half_dim = values.shape[-1] // 2
    exponent = jnp.arange(half_dim, dtype=jnp.float32) * (2.0 / values.shape[-1])
    frequency = jnp.power(jnp.float32(THETA_BASE), -exponent)
    angles = positions.astype(jnp.float32)[:, None] * frequency[None, :]
    cosine = jnp.cos(angles)[:, None, :]
    sine_part = jnp.sin(angles)[:, None, :]
    first_half = values[..., :half_dim]
    second = values[..., half_dim:]
    return jnp.concatenate([first_half * cosine - second * sine_part, second * cosine + first_half * sine_part], axis=-1)


def one_sequence(hidden, block_mask, w_query, w_key, w_value):
    positions = jnp.arange(SEQ, dtype=jnp.int32)
    query = jnp.dot(hidden, w_query, preferred_element_type=jnp.float32).reshape(SEQ, H, HD)
    key_rows = jnp.dot(hidden, w_key, preferred_element_type=jnp.float32).reshape(SEQ, KV, HD)
    value_rows = jnp.dot(hidden, w_value, preferred_element_type=jnp.float32).reshape(SEQ, KV, HD).astype(jnp.bfloat16)
    query = rotate(query, positions).astype(jnp.bfloat16)
    key_rows = rotate(key_rows, positions).astype(jnp.bfloat16)
    key_heads = jnp.repeat(key_rows, H // KV, axis=1).astype(jnp.float32)
    value_heads = jnp.repeat(value_rows, H // KV, axis=1).astype(jnp.float32)
    key_block = positions // MBLK
    score_scale = HD ** -0.5

    def tile(offset):
        query_tile = lax.dynamic_slice_in_dim(query, offset, MBLK, 0).astype(jnp.float32)
        row_pos = offset + jnp.arange(MBLK, dtype=jnp.int32)
        scores = jnp.einsum("qhd,khd->hqk", query_tile, key_heads) * score_scale
        allowed = (block_mask[row_pos // MBLK][:, key_block] > 0) & (positions[None, :] <= row_pos[:, None])
        scores = jnp.where(allowed[None], scores, -1e30)
        row_best = jnp.max(scores, axis=2, keepdims=True)
        weights = jnp.exp(scores - row_best)
        row_total = jnp.sum(weights, axis=2)
        rounded = weights.astype(jnp.bfloat16).astype(jnp.float32)
        mixed = jnp.einsum("hqk,khd->qhd", rounded, value_heads)
        return (mixed / row_total.T[:, :, None]).astype(jnp.bfloat16)

    offsets = jnp.arange(SEQ // MBLK, dtype=jnp.int32) * MBLK
    output = lax.map(tile, offsets)
    return output.reshape(SEQ, H * HD)


def reference(hidden_states, block_table, w_query, w_key, w_value):
    results = []
    for sequence in range(BATCH):
        results.append(one_sequence(hidden_states[sequence], block_table[sequence], w_query, w_key, w_value))
    return jnp.stack(results)
```

```python
import functools

import jax
import jax.numpy as jnp
from jax import lax
from jax.experimental import pallas as pl
from jax.experimental.pallas import tpu as pltpu
from jax.sharding import Mesh
from jax.sharding import PartitionSpec as P

H = 16
KV = 4
HD = 128
MBLK = 512
THETA_BASE = 500000.0
LOG2E = 1.4426950408889634

AXES = ("dp", "z", "core", "ylo", "x")
Y = ("dp", "ylo")
CX = ("core", "x")


def shift(value, axis, steps):
    count = lax.axis_size(axis)
    return lax.ppermute(value, axis, [(i, (i + steps) % count) for i in range(count)])


def put(buffer, value, index):
    return lax.dynamic_update_index_in_dim(buffer, value, index, 0)


def ring_gather(value, axis):
    rank = lax.axis_index(axis)
    half = value.shape[0] // 2
    left = shift(value, axis, 1)
    right = shift(value, axis, -1)
    far_low = shift(left[:half], axis, 1)
    far_high = shift(right[half:], axis, -1)
    out = jnp.zeros((4,) + value.shape, value.dtype)
    out = put(out, value, rank)
    out = put(out, left, (rank + 3) % 4)
    out = put(out, right, (rank + 1) % 4)
    return put(out, jnp.concatenate([far_low, far_high], axis=0), (rank + 2) % 4)


def ring_exchange(value, axis):
    rank = lax.axis_index(axis)
    out = put(jnp.zeros_like(value), lax.dynamic_index_in_dim(value, rank, 0, False), rank)
    for step in (1, 3, 2):
        piece = lax.dynamic_index_in_dim(value, (rank + step) % 4, 0, False)
        out = put(out, shift(piece, axis, step), (rank + 4 - step) % 4)
    return out


def angles(positions):
    half_dim = HD // 2
    exponent = jnp.arange(half_dim, dtype=jnp.float32) * (2.0 / HD)
    frequency = jnp.power(jnp.float32(THETA_BASE), -exponent)
    angle = positions.astype(jnp.float32)[:, None] * frequency[None, :]
    cosine, sine = jnp.cos(angle), jnp.sin(angle)
    return jnp.concatenate([cosine, cosine], axis=1), jnp.concatenate([-sine, sine], axis=1)


def project_body(parts, hid_ref, cos_ref, sin_ref, *refs):
    w_refs, out_ref, joined = refs[:-2], refs[-2], refs[-1]
    for ref, row_block, col_block, index in parts:
        joined[row_block * 256 : (row_block + 1) * 256, col_block * HD : (col_block + 1) * HD] = (
            w_refs[ref][index]
        )
    total = jnp.dot(hid_ref[...], joined[...], preferred_element_type=jnp.float32)
    for head in range(2):
        one = total[:, head * HD : (head + 1) * HD]
        turned = one * cos_ref[...] + pltpu.roll(one, HD // 2, 1) * sin_ref[...]
        out_ref[head] = turned.astype(jnp.bfloat16)


def project(hidden, cosine, sine, weights, specs, parts, steps, name):
    whole = lambda a: pl.BlockSpec(a.shape, lambda i: (0, 0))
    rows = hidden.shape[0]
    return pl.pallas_call(
        functools.partial(project_body, parts),
        grid=(steps,),
        in_specs=[whole(hidden), whole(cosine), whole(sine)] + specs,
        out_specs=pl.BlockSpec((2, rows, HD), lambda i: (i, 0, 0)),
        out_shape=jax.ShapeDtypeStruct((2 * steps, rows, HD), jnp.bfloat16),
        scratch_shapes=[pltpu.VMEM((hidden.shape[1], 2 * HD), jnp.bfloat16)],
        cost_estimate=pl.CostEstimate(
            flops=2 * rows * hidden.shape[1] * 2 * HD * steps,
            bytes_accessed=2 * (hidden.size + hidden.shape[1] * 2 * HD * steps),
            transcendentals=0,
        ),
        name=name,
    )(hidden, cosine, sine, *weights)


def attend_body(scale, info_ref, table_ref, q_ref, own_ref, other_ref, out_ref, k_all, v_all, best, total, accum, sems):
    core, z, ylo = info_ref[0], info_ref[1], info_ref[2]
    step = pl.program_id(0)
    half, par = step // 2, step % 2

    def load(first, second):
        one = pltpu.make_async_copy(first, k_all, sems.at[0])
        two = pltpu.make_async_copy(second, v_all, sems.at[1])
        one.start()
        two.start()
        one.wait()
        two.wait()

    @pl.when((step == 0) & (core == 0))
    def _():
        load(own_ref, other_ref)

    @pl.when((step == 0) & (core == 1))
    def _():
        load(other_ref, own_ref)

    mine = 8 * z + 4 * half + 2 * ylo + par

    def piece(tile, low):
        tile_z, tile_half, tile_ylo, tile_par = tile // 8, (tile // 4) % 2, (tile // 2) % 2, tile % 2
        return ((tile_z * 2 + tile_ylo) * 4 + 2 * tile_par + low) * 2 + tile_half

    k_low, k_high = k_all[piece(mine, 0)], k_all[piece(mine, 1)]
    v_low, v_high = v_all[piece(mine, 0)], v_all[piece(mine, 1)]
    contract = (((1,), (1,)), ((), ()))
    for head in range(2):
        for low in range(2):
            at = (head * 2 + low) * 256
            q_rows = q_ref[low, head, 0]
            keys = k_low if low == 0 else jnp.concatenate([k_low, k_high], axis=0)
            vals = v_low if low == 0 else jnp.concatenate([v_low, v_high], axis=0)
            scores = lax.dot_general(q_rows, keys, contract, preferred_element_type=jnp.float32)
            row = lax.broadcasted_iota(jnp.int32, scores.shape, 0) + low * 256
            col = lax.broadcasted_iota(jnp.int32, scores.shape, 1)
            scores = jnp.where(col <= row, scores, -1e30)
            new_best = jnp.max(scores, axis=1, keepdims=True)
            weights = jnp.exp2((scores - new_best) * scale)
            best[at : at + 256] = jnp.broadcast_to(new_best, (256, HD))
            part = weights[:, :HD]
            for lane in range(1, scores.shape[1] // HD):
                part = part + weights[:, lane * HD : (lane + 1) * HD]
            total[at : at + 256] = part
            accum[at : at + 256] = jnp.dot(
                weights.astype(jnp.bfloat16), vals, preferred_element_type=jnp.float32
            )

    def visit(tile, carry):
        @pl.when(table_ref[mine, tile] > 0)
        def _():
            keys = jnp.concatenate([k_all[piece(tile, 0)], k_all[piece(tile, 1)]], axis=0)
            vals = jnp.concatenate([v_all[piece(tile, 0)], v_all[piece(tile, 1)]], axis=0)
            for chunk in range(4):
                at = chunk * 256
                q_rows = q_ref[chunk % 2, chunk // 2, 0]
                scores = lax.dot_general(q_rows, keys, contract, preferred_element_type=jnp.float32)
                old_best = best[at : at + 256]
                new_best = jnp.maximum(old_best, jnp.max(scores, axis=1, keepdims=True))
                shrink = jnp.exp2((old_best - new_best) * scale)
                weights = jnp.exp2((scores - jnp.tile(new_best, (1, 4))) * scale)
                best[at : at + 256] = new_best
                part = total[at : at + 256] * shrink
                for lane in range(4):
                    part = part + weights[:, lane * HD : (lane + 1) * HD]
                total[at : at + 256] = part
                accum[at : at + 256] = accum[at : at + 256] * shrink + jnp.dot(
                    weights.astype(jnp.bfloat16), vals, preferred_element_type=jnp.float32
                )

        return carry

    lax.fori_loop(0, mine, visit, 0)

    for head in range(2):
        for low in range(2):
            at = (head * 2 + low) * 256
            row_total = jnp.sum(total[at : at + 256], axis=1, keepdims=True)
            out_ref[low, 0, :, head * HD : (head + 1) * HD] = (
                accum[at : at + 256] / row_total
            ).astype(jnp.bfloat16)


def attend(info, table, query, own, other):
    scale = HD ** (-0.5) * LOG2E
    pieces = own.shape[0]
    return pl.pallas_call(
        functools.partial(attend_body, scale),
        grid_spec=pltpu.PrefetchScalarGridSpec(
            num_scalar_prefetch=2,
            grid=(4,),
            in_specs=[
                pl.BlockSpec((2, 2, 1, 256, HD), lambda i, *_: (i % 2, 0, i // 2, 0, 0)),
                pl.BlockSpec(memory_space=pl.ANY),
                pl.BlockSpec(memory_space=pl.ANY),
            ],
            out_specs=pl.BlockSpec((2, 1, 256, 2 * HD), lambda i, *_: (i % 2, i // 2, 0, 0)),
            scratch_shapes=[
                pltpu.VMEM((pieces, 256, HD), jnp.bfloat16),
                pltpu.VMEM((pieces, 256, HD), jnp.bfloat16),
                pltpu.VMEM((1024, HD), jnp.float32),
                pltpu.VMEM((1024, HD), jnp.float32),
                pltpu.VMEM((1024, HD), jnp.float32),
                pltpu.SemaphoreType.DMA((2,)),
            ],
        ),
        out_shape=jax.ShapeDtypeStruct((4, 2, 256, 2 * HD), jnp.bfloat16),
        cost_estimate=pl.CostEstimate(flops=20_000_000_000, bytes_accessed=12 << 20, transcendentals=40_000_000),
        name="attend",
    )(info, table, query, own, other)


def shards(hidden_states, block_table, w_query, w_key, w_value):
    core, z, ylo, x = (lax.axis_index(a) for a in ("core", "z", "ylo", "x"))
    flip = [(0, 1), (1, 0)]
    own_rows = hidden_states[0]

    keep = lax.dynamic_slice_in_dim(w_query, core * HD, HD, 1)
    give = lax.dynamic_slice_in_dim(w_query, (1 - core) * HD, HD, 1)
    got = lax.ppermute(give, "core", flip)
    first = jnp.where(core == 0, keep, got)
    second = jnp.where(core == 0, got, keep)

    low = x % 2
    spot = lambda c, j, b: c * 4 + 2 * j + b
    straight = [(spot(a, j, b), spot(b, j, a)) for a in range(2) for j in range(2) for b in range(2)]
    crossed = [(spot(a, j, b), spot(1 - b, j, a)) for a in range(2) for j in range(2) for b in range(2)]
    got_straight = lax.ppermute(jnp.where(low == 0, w_key, w_value), CX, straight)
    got_crossed = lax.ppermute(jnp.where(low == 0, w_value, w_key), CX, crossed)
    third = jnp.where(
        core == 0,
        jnp.concatenate([got_straight, got_crossed], axis=1),
        jnp.concatenate([got_crossed, got_straight], axis=1),
    )

    other_rows = lax.ppermute(own_rows, "core", flip)
    hidden = jnp.concatenate(
        [jnp.where(core == 0, own_rows, other_rows), jnp.where(core == 0, other_rows, own_rows)], axis=0
    )

    def gather(value, axes):
        for axis in axes:
            value = ring_gather(value, axis).reshape(-1, HD)
        return value

    w_first = gather(first, ("x", Y, "z")).reshape(4, 2, 2, 4, 256, HD)
    w_second = gather(second, (Y, "z", "x")).reshape(4, 4, 2, 2, 256, HD)
    w_third = gather(third, ("z", "x", Y)).reshape(2, 2, 4, 4, 256, HD)

    token = jnp.arange(256, dtype=jnp.int32)
    positions = (((2 * z + jnp.arange(2, dtype=jnp.int32)) * 8 + ylo * 4 + x)[:, None] * 256 + token[None, :]).reshape(-1)
    cosine, sine = angles(positions)
    kv_cosine = jnp.where(core == 0, cosine, 1.0)
    kv_sine = jnp.where(core == 0, sine, 0.0)

    kv_parts = [
        (0, (dp * 4 + zz) * 2 + xl, xh, (dp, 0, 2 * xh + xl, zz))
        for dp in range(2)
        for zz in range(4)
        for xl in range(2)
        for xh in range(2)
    ]
    kv_spec = pl.BlockSpec((2, 1, 4, 4, 256, HD), lambda i: (0, i, 0, 0, 0, 0))
    kv_mine = project(hidden, kv_cosine, kv_sine, [w_third], [kv_spec], kv_parts, 2, "project_kv")

    q_parts = []
    for dp in range(2):
        for zz in range(4):
            for k in range(2):
                q_parts.append((0, (dp * 4 + zz) * 2, k, (zz, dp, 0, k)))
                q_parts.append((1, (dp * 4 + zz) * 2 + 1, k, (k, zz, dp, 0)))
    q_specs = [
        pl.BlockSpec((4, 2, 1, 2, 256, HD), lambda i: (0, 0, i // 2, i % 2, 0, 0)),
        pl.BlockSpec((2, 4, 2, 1, 256, HD), lambda i: (i % 2, 0, 0, i // 2, 0, 0)),
    ]
    q_mine = project(hidden, cosine, sine, [w_first, w_second], q_specs, q_parts, 4, "project_q")

    kv_tokens = ring_exchange(kv_mine, "x").reshape(8, 256, HD)
    kv_other = lax.ppermute(kv_tokens, "ylo", flip)
    kv_pair = put(put(jnp.zeros((2, 8, 256, HD), jnp.bfloat16), kv_tokens, ylo), kv_other, 1 - ylo)
    kv_own = ring_gather(kv_pair.reshape(16, 256, HD), "z").reshape(64, 256, HD)
    kv_partner = lax.ppermute(kv_own, "core", flip)

    query = ring_exchange(q_mine.reshape(4, 2 * 512, HD), "x").reshape(4, 2, 2, 256, HD)

    info = jnp.stack([core, z, ylo]).astype(jnp.int32)
    mixed = attend(info, block_table[0], query, kv_own, kv_partner)

    rank = core * 4 + x
    out = jnp.zeros((8, 256, 2 * HD), jnp.bfloat16)
    out = put(out, lax.dynamic_index_in_dim(mixed[:, :], x, 0, False)[core], rank)
    by_source = mixed.transpose(1, 0, 2, 3).reshape(8, 256, 2 * HD)
    for dc in range(2):
        for dx in range(4):
            if dc == 0 and dx == 0:
                continue
            pairs = [(c * 4 + s, ((c + dc) % 2) * 4 + (s + dx) % 4) for c in range(2) for s in range(4)]
            to = ((core + dc) % 2) * 4 + (x + dx) % 4
            source = ((core + dc) % 2) * 4 + (x + 4 - dx) % 4
            piece = lax.dynamic_index_in_dim(by_source, to, 0, False)
            out = put(out, lax.ppermute(piece, CX, pairs), source)
    out = out.reshape(2, 4, 256, 2, HD).transpose(2, 1, 3, 0, 4).reshape(256, H * HD)
    return out[None]


def solution(mesh):
    fine = Mesh(mesh.devices.reshape(2, 4, 2, 2, 4), AXES)
    blk, uly = ("z", "core"), ("ylo", "x")
    weight = P(("dp",) + blk, uly)
    placed = (P("dp", blk + uly, None), P("dp", None, None), weight, weight, weight)
    return jax.shard_map(
        shards, mesh=fine, in_specs=placed, out_specs=P("dp", blk + uly, None), check_vma=False
    )
```
